32 devices in a mesh: tm: 8 (over y, x, core), space: 4 (over z).
Axes of the slice: x: 2, y: 2, z: 4, core: 2. Of those that a mesh axis runs over, the one named last changes fastest.
Arguments:
- coarse_guess: float32 [8, 32, 12, 512], P('tm', 'space'), may hold values from -6 to 6
- initial_state: float32 [32, 12, 512], P('space'), may hold values from -6 to 6
- fine_volume: bfloat16 [512, 512], replicated
- coarse_volume: bfloat16 [512, 512], replicated
- lift_matrix: bfloat16 [384, 512], replicated, may hold values from -0.0390625 to 0.0390625
- wave_speed: float32 [12], replicated, may hold values from 0.1 to 0.6
- reaction_rate: float32 [24], replicated, may hold values from 0.05 to 0.5
- species_map: int32 [24, 3], replicated, may hold values from 0 to 11
- neighbour_element: int32 [32, 6], P('space'), may hold values from 0 to 7
- neighbour_rank: int32 [32, 6], P('space'), may hold values from -1 to 1
Outputs:
- iterate: float32 [32, 32, 12, 512], P('tm', 'space')
The draws below stay inside these ranges and needn't reach their ends.
All inputs are finite; a program needn't handle non-finite values.
Results may differ from the reference program's by a relative error of at most 0.025.
Values may be sent and summed in bfloat16 or wider, within the bound.
A program may use at most 64 MiB of HBM per device.

```python
import math
import jax
import jax.numpy as jnp
from jax import lax

SIDE = 8
NODES = 512
FACE_NODES = 384
VARS = 12
REACTIONS = 24
STRIDE = 4
E_DEV = 8
ELEMS = 32
NT = 32
N_TM = 8
N_SPACE = 4


def operator_draw(key, lower, upper, rough):
    diagonal = jax.random.uniform(jax.random.fold_in(key, 11), (NODES,), jnp.float32, lower, upper)
    return (jnp.diag(diagonal) + rough * (0.15 / math.sqrt(NODES))).astype(jnp.bfloat16)


def draw_fine_volume(key, part):
    inner = jax.random.fold_in(key, 101)
    rough = jax.random.normal(jax.random.fold_in(inner, 3), (NODES, NODES), jnp.float32)
    return operator_draw(inner, 0.45, 0.7, rough)


def draw_coarse_volume(key, part):
    inner = jax.random.fold_in(key, 202)
    rough = jax.random.normal(jax.random.fold_in(inner, 3), (NODES, NODES), jnp.float32)
    return operator_draw(inner, 0.35, 0.6, rough)


def with_ends(array, own_key, least, high):
    longest = array.shape.index(max(array.shape))
    spots = []
    for shift in (0, 1):
        where = [jax.random.randint(jax.random.fold_in(own_key, axis), (), 0, length) for axis, length in enumerate(array.shape)]
        where[longest] = (where[longest] + shift) % array.shape[longest]
        spots.append(tuple(where))
    return array.at[spots[0]].set(least).at[spots[1]].set(high)


def steps_of(rng, extent, shards, low, top_value):
    def one(axis_at, shards_of):
        steps = jax.random.uniform(jax.random.fold_in(jax.random.fold_in(rng, 6), axis_at), (shards_of,), jnp.float32, low / len(shards), top_value / len(shards))
        return jnp.repeat(jnp.exp(steps), extent[axis_at] // shards_of).reshape((-1,) + (1,) * (len(extent) - axis_at - 1))

    level = one(*shards[0])
    for cut in shards[1:]:
        level = level * one(*cut)
    return level


def scatter_about(own_key, extent, scale, most, shards=(), kind=jnp.bfloat16):
    entries = scale * jax.random.normal(own_key, extent, jnp.float32)
    if shards:
        entries = entries * steps_of(own_key, extent, shards, -0.22, 0.18)
    return jnp.clip(entries, -most, most).astype(kind)


def setup_inputs(seed: int = 0) -> dict:
    key_list = jax.random.split(jax.random.key(seed), 11)
    coarse_guess = scatter_about(key_list[0], (N_TM, ELEMS, VARS, NODES), 1.0, 6.0, ((0, 8), (1, 4)), jnp.float32)
    initial_state = scatter_about(key_list[1], (ELEMS, VARS, NODES), 1.0, 6.0, ((0, 4),), jnp.float32)
    fine_volume = draw_fine_volume(jax.random.fold_in(key_list[10], 71), 0)
    coarse_volume = draw_coarse_volume(jax.random.fold_in(key_list[10], 71), 0)
    lift_matrix = scatter_about(key_list[4], (FACE_NODES, NODES), (64 * FACE_NODES) ** -0.5, 0.0390625)
    wave_speed = jnp.clip(jnp.exp(jax.random.uniform(key_list[5], (VARS,), jnp.float32, math.log(0.1), math.log(0.6))), 0.1, 0.6)
    reaction_rate = jnp.clip(jnp.exp(jax.random.uniform(key_list[6], (REACTIONS,), jnp.float32, math.log(0.05), math.log(0.5))), 0.05, 0.5)
    species_map = with_ends(jax.random.randint(key_list[7], (REACTIONS, 3), 0, VARS), jax.random.fold_in(key_list[7], 1), 0, VARS - 1).astype(jnp.int32)
    neighbour_element = with_ends(jax.random.randint(key_list[8], (ELEMS, 6), 0, E_DEV), jax.random.fold_in(key_list[8], 1), 0, E_DEV - 1).astype(jnp.int32)
    neighbour_rank = with_ends(jax.random.randint(key_list[9], (ELEMS, 6), -1, 2), jax.random.fold_in(key_list[9], 1), -1, 1).astype(jnp.int32)
    return dict(coarse_guess=coarse_guess, initial_state=initial_state, fine_volume=fine_volume, coarse_volume=coarse_volume, lift_matrix=lift_matrix, wave_speed=wave_speed, reaction_rate=reaction_rate, species_map=species_map, neighbour_element=neighbour_element, neighbour_rank=neighbour_rank)


coarse_gain = 4.0


def face_cut(rounded):
    blocked = rounded.reshape(rounded.shape[:-1] + (SIDE, SIDE, SIDE))
    planes = [blocked[..., 0, :, :], blocked[..., -1, :, :], blocked[..., :, 0, :],
              blocked[..., :, -1, :], blocked[..., :, :, 0], blocked[..., :, :, -1]]
    return jnp.stack([plane.reshape(rounded.shape[:-1] + (SIDE * SIDE,)) for plane in planes], axis=-2)


def selections(species_map):
    labels = jnp.arange(VARS, dtype=jnp.int32)[None, :]
    first_table = (species_map[:, 0:1] == labels).astype(jnp.float32)
    second_table = (species_map[:, 1:2] == labels).astype(jnp.float32)
    made_table = (species_map[:, 2:3] == labels).astype(jnp.float32)
    return first_table, second_table, made_table - first_table


def react(state, tables, scaled_rates):
    first_table, second_table, change_table = tables
    first_amount = jnp.einsum('rv,...vn->...rn', first_table, state, precision=lax.Precision.HIGHEST)
    second_amount = jnp.einsum('rv,...vn->...rn', second_table, state, precision=lax.Precision.HIGHEST)
    speed_term = scaled_rates[:, None] * first_amount * second_amount / (
        1.0 + first_amount * first_amount + second_amount * second_amount)
    return state + jnp.einsum('rv,...rn->...vn', change_table, speed_term, precision=lax.Precision.HIGHEST)


def reference(coarse_guess, initial_state, fine_volume, coarse_volume, lift_matrix, wave_speed,
              reaction_rate, species_map, neighbour_element, neighbour_rank):
    tables = selections(species_map)
    home_block = (jnp.arange(ELEMS, dtype=jnp.int32) // E_DEV)[:, None]
    partner = (((home_block + neighbour_rank) % N_SPACE) * E_DEV + neighbour_element).astype(jnp.int32)

    def substep(state, volume, gain):
        rounded = state.astype(jnp.bfloat16)
        own_faces = face_cut(rounded)
        across = jnp.stack([jnp.take(own_faces[..., which_face ^ 1, :], partner[:, which_face], axis=-3)
                            for which_face in range(6)], axis=-2)
        jumps = (wave_speed[:, None, None] * (across.astype(jnp.float32) - own_faces.astype(jnp.float32)))
        jumps = jumps.astype(jnp.bfloat16).reshape(state.shape[:-1] + (FACE_NODES,))
        moved = jnp.dot(rounded, volume, preferred_element_type=jnp.float32)
        moved = moved + jnp.dot(jumps, lift_matrix, preferred_element_type=jnp.float32)
        return react(moved, tables, reaction_rate * gain)

    def fine_step(state):
        return substep(substep(state, fine_volume, 1.0), fine_volume, 1.0)

    def coarse_step(state):
        return substep(state, coarse_volume, coarse_gain)

    def relax(starts):
        points = []
        current = starts
        for number in range(STRIDE - 1):
            current = fine_step(current)
            points.append(current)
        return points

    starts = jnp.concatenate([initial_state[None], coarse_guess[1:]], axis=0)
    relaxed = fine_step(relax(starts)[-1])
    second = jnp.concatenate([initial_state[None], relaxed[:-1]], axis=0)
    correction = fine_step(relax(second)[-1]) - coarse_step(second)

    def chain(value, term):
        updated = coarse_step(value) + term
        return updated, updated

    final_value, coarse_values = lax.scan(chain, initial_state, correction)
    third = jnp.concatenate([initial_state[None], coarse_values[:-1]], axis=0)
    points = relax(third) + [coarse_values]
    stacked = jnp.stack(points, axis=1)
    return stacked.reshape((NT, ELEMS, VARS, NODES))
```

```python
import functools

import jax
import jax.numpy as jnp
import numpy as np
from jax import lax
from jax.experimental import pallas as pl
from jax.experimental.pallas import tpu as pltpu
from jax.sharding import PartitionSpec as P

SIDE = 8
STRIDE = 4
COARSE_GAIN = 4.0
VMEM = pltpu.VMEM
SMEM = pltpu.SMEM
MESH = pl.DeviceIdType.MESH


def face_tables(side):
    plane = side * side
    inner = np.arange(plane)
    first, second = inner // side, inner % side
    last = side - 1
    node_lists = [
        first * side + second,
        last * plane + first * side + second,
        first * plane + second,
        first * plane + last * side + second,
        first * plane + second * side,
        first * plane + second * side + last,
    ]
    table = np.zeros((side**3, 12 * plane), np.float32)
    for f in range(6):
        table[node_lists[f], f * plane + inner] = 1.0
        table[node_lists[f ^ 1], (6 + f) * plane + inner] = 1.0
    return table


def find_jumps(speed, c, x_ref, g_ref, j_ref):
    variables = speed.shape[0]
    elems = x_ref.shape[0] // variables
    faces = c["table"].shape[1] // 2
    plane = faces // 6
    pair = 2 * plane
    both = jnp.dot(x_ref[...], c["table"][...], preferred_element_type=jnp.float32)
    lane = lax.broadcasted_iota(jnp.int32, (1, pair), 1)
    low = jnp.where(lane < plane, 1.0, 0.0)
    high = 1.0 - low
    for k in range(3):
        for v in range(variables):
            rows = slice(v * elems, (v + 1) * elems)
            swapped = both[rows, faces + k * pair : faces + (k + 1) * pair]
            cols = slice(v * pair, (v + 1) * pair)
            g_ref[k, 0:elems, cols] = (swapped * low).astype(jnp.bfloat16)
            g_ref[k, elems : 2 * elems, cols] = (swapped * high).astype(jnp.bfloat16)
    for k in range(3):
        across = jnp.dot(c["pick"][k], g_ref[k], preferred_element_type=jnp.float32)
        for v in range(variables):
            rows = slice(v * elems, (v + 1) * elems)
            own = both[rows, k * pair : (k + 1) * pair]
            jump = speed[v] * (across[:, v * pair : (v + 1) * pair] - own)
            j_ref[rows, k * pair : (k + 1) * pair] = jump.astype(jnp.bfloat16)


def transport_react(gain, volume, c, x_ref, j_ref, m_ref, a_ref):
    variables, elems, nodes = m_ref.shape
    moved = jnp.dot(x_ref[...], volume[...], preferred_element_type=jnp.float32)
    moved = moved + jnp.dot(j_ref[...], c["lift"][...], preferred_element_type=jnp.float32)
    moved = moved.reshape(m_ref.shape)
    m_ref[...] = moved
    a_ref[...] = moved
    species, rates = c["species"], c["rates"]
    for r in range(species.shape[0]):
        s0, s1, s2 = species[r, 0], species[r, 1], species[r, 2]
        a, b = m_ref[s0], m_ref[s1]
        rate = (rates[r] * gain) * (a * b) / (1.0 + a * a + b * b)
        a_ref[s2] += rate
        a_ref[s0] -= rate


def store_state(a_ref, x_ref):
    x_ref[...] = a_ref[...].reshape(x_ref.shape).astype(jnp.bfloat16)


CONSTS = ("table", "pick", "lift", "fine", "coarse", "speed", "rates", "species")
IN_SMEM = ("speed", "rates", "species")


def phase_scratch(variables, elems, nodes, faces):
    return [
        VMEM((variables * elems, nodes), jnp.bfloat16),
        VMEM((3, 2 * elems, variables * (faces // 3)), jnp.bfloat16),
        VMEM((variables * elems, faces), jnp.bfloat16),
        VMEM((variables, elems, nodes), jnp.float32),
        VMEM((variables, elems, nodes), jnp.float32),
    ]


def fine_substep(c, x, g, j, m, a):
    find_jumps(c["speed"], c, x, g, j)
    transport_react(1.0, c["fine"], c, x, j, m, a)
    store_state(a, x)


def loop(count, fn):
    def one(i, carry):
        fn(i)
        return carry

    lax.fori_loop(0, count, one, 0)


def phase_one(*refs):
    c = dict(zip(CONSTS, refs))
    start, out = refs[len(CONSTS) : len(CONSTS) + 2]
    x, g, j, m, a = refs[len(CONSTS) + 2 :]
    x[...] = start[...].reshape(x.shape)
    loop(2 * STRIDE, lambda i: fine_substep(c, x, g, j, m, a))
    out[...] = x[...].reshape(out.shape)


def phase_two(*refs):
    c = dict(zip(CONSTS, refs))
    row, second, corr, message = refs[len(CONSTS) : len(CONSTS) + 4]
    x, g, j, m, a = refs[len(CONSTS) + 4 :]
    x[...] = second[...].reshape(x.shape)
    find_jumps(c["speed"], c, x, g, j)
    transport_react(COARSE_GAIN, c["coarse"], c, x, j, m, a)
    corr[...] = a[...]
    loop(2 * STRIDE, lambda i: fine_substep(c, x, g, j, m, a))
    keep = jnp.where(row[0] == 1, 0.0, 1.0)
    message[...] = (a[...] - keep * corr[...]).astype(jnp.bfloat16)
    corr[...] = a[...] - corr[...]


def phase_three(*refs):
    c = dict(zip(CONSTS, refs))
    row, second, corr, messages, out = refs[len(CONSTS) : len(CONSTS) + 5]
    x, g, j, m, a = refs[len(CONSTS) + 5 :]
    here = row[0]
    block = out.shape[2]
    own = pl.ds(pl.multiple_of(row[1] * block, block), block)

    @pl.when(here < 2)
    def _():
        x[...] = second[...].reshape(x.shape)

    @pl.when(here >= 2)
    def _():
        x[...] = messages[1].reshape(x.shape)

    def coarse():
        find_jumps(c["speed"], c, x, g, j)
        transport_react(COARSE_GAIN, c["coarse"], c, x, j, m, a)

    def advance(i, carry):
        coarse()
        a[...] += messages[i].astype(jnp.float32)
        store_state(a, x)
        return carry

    lax.fori_loop(2, here, advance, 0)
    coarse()
    out[STRIDE - 1] = a[:, own, :] + corr[:, own, :]

    def point(k):
        loop(2, lambda i: fine_substep(c, x, g, j, m, a))
        out[k] = a[:, own, :]

    loop(STRIDE - 1, point)


def barrier_with(axis, offsets):
    me, size = lax.axis_index(axis), lax.axis_size(axis)
    barrier = pltpu.get_barrier_semaphore()
    for d in offsets:
        pl.semaphore_signal(
            barrier, inc=1, device_id={axis: lax.rem(me + d, size)}, device_id_type=MESH
        )
    pl.semaphore_wait(barrier, len(offsets))


def gather_kernel(axis, count, *refs):
    ins, outs = refs[:count], refs[count : 2 * count]
    send, recv, local = refs[2 * count :]
    me, size = lax.axis_index(axis), lax.axis_size(axis)
    barrier_with(axis, range(1, size))
    copies = []
    for d in range(1, size):
        for i in range(count):
            copies.append(
                pltpu.make_async_remote_copy(
                    src_ref=ins[i],
                    dst_ref=outs[i].at[me],
                    send_sem=send.at[i, d - 1],
                    recv_sem=recv.at[i, d - 1],
                    device_id={axis: lax.rem(me + d, size)},
                    device_id_type=MESH,
                )
            )
            copies[-1].start()
    for i in range(count):
        mine = pltpu.make_async_copy(ins[i], outs[i].at[me], local.at[i])
        mine.start()
        copies.append(mine)
    for copy in copies:
        copy.wait()


def gather(axis, arrays, cid):
    size, count = lax.axis_size(axis), len(arrays)
    return pl.pallas_call(
        functools.partial(gather_kernel, axis, count),
        out_shape=[jax.ShapeDtypeStruct((size,) + x.shape, x.dtype) for x in arrays],
        in_specs=[pl.BlockSpec(memory_space=VMEM)] * count,
        out_specs=[pl.BlockSpec(memory_space=VMEM)] * count,
        scratch_shapes=[
            pltpu.SemaphoreType.DMA((count, size - 1)),
            pltpu.SemaphoreType.DMA((count, size - 1)),
            pltpu.SemaphoreType.DMA((count,)),
        ],
        compiler_params=pltpu.CompilerParams(collective_id=cid, has_side_effects=True),
    )(*arrays)


def run_phase(kernel, consts, scalars, arrays, out_shape, scratch):
    smem, vmem = pl.BlockSpec(memory_space=SMEM), pl.BlockSpec(memory_space=VMEM)
    specs = [smem if name in IN_SMEM else vmem for name in CONSTS]
    specs += [smem] * len(scalars) + [vmem] * len(arrays)
    return pl.pallas_call(
        kernel,
        out_shape=out_shape,
        in_specs=specs,
        out_specs=jax.tree.map(lambda _: vmem, out_shape),
        scratch_shapes=scratch,
        compiler_params=pltpu.CompilerParams(vmem_limit_bytes=60 * 1024 * 1024),
    )(*consts, *scalars, *arrays)


def constants(partner, fine_volume, coarse_volume, lift, speed, rates, species):
    elems = partner.shape[0]
    labels = jnp.arange(elems, dtype=jnp.int32)
    hot = (partner[:, :, None] == labels).astype(jnp.bfloat16)
    pick = jnp.transpose(hot.reshape(elems, 3, 2 * elems), (1, 0, 2))
    table = jnp.asarray(face_tables(SIDE)).astype(jnp.bfloat16)
    return (table, pick, lift, fine_volume, coarse_volume, speed, rates, species)


def body(
    coarse_guess,
    initial_state,
    fine_volume,
    coarse_volume,
    lift_matrix,
    wave_speed,
    reaction_rate,
    species_map,
    neighbour_element,
    neighbour_rank,
):
    block, variables, nodes = initial_state.shape
    blocks = lax.axis_size("space")
    elems = block * blocks
    row, col = lax.axis_index("tm"), lax.axis_index("space")
    start = jnp.where(row == 0, initial_state, coarse_guess[0]).astype(jnp.bfloat16)
    partner = jnp.mod(col + neighbour_rank, blocks) * block + neighbour_element
    partner = jnp.pad(partner, ((0, 0), (0, 128 - partner.shape[1])))
    starts, partners = gather("space", [start, partner], 0)
    starts = jnp.transpose(starts.reshape(elems, variables, nodes), (1, 0, 2))
    partners = partners.reshape(elems, 128)[:, :6]
    consts = constants(
        partners, fine_volume, coarse_volume, lift_matrix, wave_speed, reaction_rate, species_map
    )
    scratch = phase_scratch(variables, elems, nodes, lift_matrix.shape[0])
    whole = (variables, elems, nodes)
    half = jax.ShapeDtypeStruct(whole, jnp.bfloat16)
    full = jax.ShapeDtypeStruct(whole, jnp.float32)
    relaxed = run_phase(phase_one, consts, (), (starts,), half, scratch)
    rows = lax.axis_size("tm")
    received = lax.ppermute(relaxed, "tm", [(i, i + 1) for i in range(rows - 1)])
    second = jnp.where(row == 0, starts, received)
    where = jnp.stack([row, col]).astype(jnp.int32)
    corr, message = run_phase(phase_two, consts, (where,), (second,), [full, half], scratch)
    (messages,) = gather("tm", [message], 1)
    out = run_phase(
        phase_three,
        consts,
        (where,),
        (second, corr, messages),
        jax.ShapeDtypeStruct((STRIDE, variables, block, nodes), jnp.float32),
        scratch,
    )
    return jnp.transpose(out, (0, 2, 1, 3))


def solution(mesh):
    placed = (
        P("tm", "space", None, None),
        P("space", None, None),
        P(),
        P(),
        P(),
        P(),
        P(),
        P(),
        P("space", None),
        P("space", None),
    )
    return jax.shard_map(
        body, mesh=mesh, in_specs=placed, out_specs=P("tm", "space", None, None), check_vma=False
    )
```

```python
import functools

import jax
import jax.numpy as jnp
import numpy as np
from jax import lax
from jax.experimental import pallas as pl
from jax.experimental.pallas import tpu as pltpu
from jax.sharding import PartitionSpec as P

SIDE = 8
STRIDE = 4
COARSE_GAIN = 4.0
VMEM = pltpu.VMEM
SMEM = pltpu.SMEM
MESH = pl.DeviceIdType.MESH


def face_tables(side):
    plane = side * side
    inner = np.arange(plane)
    first, second = inner // side, inner % side
    last = side - 1
    node_lists = [
        first * side + second,
        last * plane + first * side + second,
        first * plane + second,
        first * plane + last * side + second,
        first * plane + second * side,
        first * plane + second * side + last,
    ]
    table = np.zeros((side**3, 12 * plane), np.float32)
    for f in range(6):
        table[node_lists[f], f * plane + inner] = 1.0
        table[node_lists[f ^ 1], (6 + f) * plane + inner] = 1.0
    return table


def find_jumps(speed, c, x_ref, g_ref, j_ref, dims):
    blocks, variables, block, _ = dims
    elems = blocks * block
    faces = c["table"].shape[1] // 2
    plane = faces // 6
    pair = 2 * plane
    both = jnp.dot(x_ref[...], c["table"][...], preferred_element_type=jnp.float32)
    lane = lax.broadcasted_iota(jnp.int32, (1, pair), 1)
    low = jnp.where(lane < plane, 1.0, 0.0)
    high = 1.0 - low

    def first_row(s, v):
        return (s * variables + v) * block

    for k in range(3):
        for v in range(variables):
            swapped = jnp.concatenate(
                [
                    both[
                        first_row(s, v) : first_row(s, v) + block,
                        faces + k * pair : faces + (k + 1) * pair,
                    ]
                    for s in range(blocks)
                ],
                axis=0,
            )
            cols = slice(v * pair, (v + 1) * pair)
            g_ref[k, 0:elems, cols] = (swapped * low).astype(jnp.bfloat16)
            g_ref[k, elems : 2 * elems, cols] = (swapped * high).astype(jnp.bfloat16)
    for k in range(3):
        across = jnp.dot(c["pick"][k], g_ref[k], preferred_element_type=jnp.float32)
        for s in range(blocks):
            for v in range(0, variables, 2):
                parts = []
                for w in (v, v + 1):
                    rows = first_row(s, w)
                    own = both[rows : rows + block, k * pair : (k + 1) * pair]
                    other = across[s * block : (s + 1) * block, w * pair : (w + 1) * pair]
                    parts.append(speed[w] * (other - own))
                rows = first_row(s, v)
                j_ref[rows : rows + 2 * block, k * pair : (k + 1) * pair] = jnp.concatenate(
                    parts, axis=0
                ).astype(jnp.bfloat16)


def transport_react(gain, volume, c, x_ref, j_ref, m_ref, a_ref):
    moved = jnp.dot(x_ref[...], volume[...], preferred_element_type=jnp.float32)
    moved = moved + jnp.dot(j_ref[...], c["lift"][...], preferred_element_type=jnp.float32)
    moved = moved.reshape(m_ref.shape)
    m_ref[...] = moved
    a_ref[...] = moved
    species, rates = c["species"], c["rates"]
    for r in range(species.shape[0]):
        s0, s1, s2 = species[r, 0], species[r, 1], species[r, 2]
        a, b = m_ref[:, s0], m_ref[:, s1]
        rate = (rates[r] * gain) * (a * b) / (1.0 + a * a + b * b)
        a_ref[:, s2] += rate
        a_ref[:, s0] -= rate


def store_state(a_ref, x_ref):
    x_ref[...] = a_ref[...].reshape(x_ref.shape).astype(jnp.bfloat16)


CONSTS = ("table", "partner", "lift", "fine", "coarse", "speed", "rates", "species")
IN_SMEM = ("speed", "rates", "species")


def phase_scratch(dims, faces):
    blocks, variables, block, nodes = dims
    rows, elems = blocks * variables * block, blocks * block
    return [
        VMEM((3, elems, 2 * elems), jnp.bfloat16),
        VMEM((rows, nodes), jnp.bfloat16),
        VMEM((3, 2 * elems, variables * (faces // 3)), jnp.bfloat16),
        VMEM((rows, faces), jnp.bfloat16),
        VMEM(dims, jnp.float32),
        VMEM(dims, jnp.float32),
    ]


def make_pick(partner_ref, pick_ref):
    _, elems, wide = pick_ref.shape
    partner = partner_ref[...].reshape(elems, partner_ref.shape[-1])
    lane = lax.broadcasted_iota(jnp.int32, (elems, wide), 1)
    for k in range(3):
        wanted = jnp.where(
            lane < elems, partner[:, 2 * k : 2 * k + 1], partner[:, 2 * k + 1 : 2 * k + 2] + elems
        )
        pick_ref[k] = jnp.where(lane == wanted, 1.0, 0.0).astype(jnp.bfloat16)


def begin(refs, count):
    c = dict(zip(CONSTS, refs))
    others = refs[len(CONSTS) : len(CONSTS) + count]
    scratch = refs[len(CONSTS) + count :]
    c["pick"] = scratch[0]
    make_pick(c["partner"], c["pick"])
    return c, others, scratch[1:]


def fine_substep(c, x, g, j, m, a):
    find_jumps(c["speed"], c, x, g, j, m.shape)
    transport_react(1.0, c["fine"], c, x, j, m, a)
    store_state(a, x)


def loop(count, fn):
    def one(i, carry):
        fn(i)
        return carry

    lax.fori_loop(0, count, one, 0)


def phase_one(*refs):
    c, (start, out), (x, g, j, m, a) = begin(refs, 2)
    x[...] = start[...].reshape(x.shape)
    loop(2 * STRIDE, lambda i: fine_substep(c, x, g, j, m, a))
    out[...] = x[...].reshape(out.shape)


def phase_two(*refs):
    c, (row, second, corr, message), (x, g, j, m, a) = begin(refs, 4)
    x[...] = second[...].reshape(x.shape)
    find_jumps(c["speed"], c, x, g, j, m.shape)
    transport_react(COARSE_GAIN, c["coarse"], c, x, j, m, a)
    corr[...] = a[...]
    loop(2 * STRIDE, lambda i: fine_substep(c, x, g, j, m, a))
    keep = jnp.where(row[0] == 1, 0.0, 1.0)
    message[...] = (a[...] - keep * corr[...]).reshape(message.shape).astype(jnp.bfloat16)
    corr[...] = a[...] - corr[...]


def phase_three(*refs):
    c, (row, second, corr, messages, out), (x, g, j, m, a) = begin(refs, 5)
    here, own = row[0], row[1]

    @pl.when(here < 2)
    def _():
        x[...] = second[...].reshape(x.shape)

    @pl.when(here >= 2)
    def _():
        x[...] = messages[1].reshape(x.shape)

    def coarse():
        find_jumps(c["speed"], c, x, g, j, m.shape)
        transport_react(COARSE_GAIN, c["coarse"], c, x, j, m, a)

    def advance(i, carry):
        coarse()
        x[...] = (
            a[...].reshape(x.shape) + messages[i].reshape(x.shape).astype(jnp.float32)
        ).astype(jnp.bfloat16)
        return carry

    lax.fori_loop(2, here, advance, 0)
    coarse()
    out[STRIDE - 1] = a[own] + corr[own]

    def point(k):
        loop(2, lambda i: fine_substep(c, x, g, j, m, a))
        out[k] = a[own]

    loop(STRIDE - 1, point)


def greet(axis):
    me, size = lax.axis_index(axis), lax.axis_size(axis)
    barrier = pltpu.get_barrier_semaphore()
    for d in range(1, size):
        pl.semaphore_signal(
            barrier, inc=1, device_id={axis: lax.rem(me + d, size)}, device_id_type=MESH
        )
    pl.semaphore_wait(barrier, size - 1)


def remote(src, dst, send, recv, axis, target):
    return pltpu.make_async_remote_copy(
        src_ref=src,
        dst_ref=dst,
        send_sem=send,
        recv_sem=recv,
        device_id={axis: target},
        device_id_type=MESH,
    )


def start_kernel(guess, initial, partner, starts, partners, mine, send, recv, local):
    me, size = lax.axis_index("space"), lax.axis_size("space")
    block, variables, _ = initial.shape
    first = lax.axis_index("tm") == 0

    def take(ref):
        for v in range(0, variables, 2):
            both = jnp.concatenate([ref[:, v, :], ref[:, v + 1, :]], axis=0)
            mine[v * block : (v + 2) * block, :] = both.astype(jnp.bfloat16)

    @pl.when(first)
    def _():
        take(initial)

    @pl.when(jnp.logical_not(first))
    def _():
        take(guess.at[0])

    greet("space")
    pairs = ((mine, starts), (partner, partners))
    copies = []
    for d in range(1, size):
        for i, (src, dst) in enumerate(pairs):
            copies.append(
                remote(
                    src,
                    dst.at[me],
                    send.at[i, d - 1],
                    recv.at[i, d - 1],
                    "space",
                    lax.rem(me + d, size),
                )
            )
            copies[-1].start()
    for i, (src, dst) in enumerate(pairs):
        copies.append(pltpu.make_async_copy(src, dst.at[me], local.at[i]))
        copies[-1].start()
    for copy in copies:
        copy.wait()


def shift_kernel(relaxed, starts, second, send, recv, local):
    me, size = lax.axis_index("tm"), lax.axis_size("tm")
    blocks = relaxed.shape[0]
    greet("tm")

    def copy(q):
        target = lax.rem(me + 1, size)
        return remote(relaxed.at[q], second.at[q], send.at[q], recv.at[q], "tm", target)

    keep = pltpu.make_async_copy(starts, second, local)

    @pl.when(me < size - 1)
    def _():
        for q in range(blocks):
            copy(q).start()

    @pl.when(me == 0)
    def _():
        keep.start()
        keep.wait()

    @pl.when(me > 0)
    def _():
        for q in range(blocks):
            copy(q).wait_recv()

    @pl.when(me < size - 1)
    def _():
        for q in range(blocks):
            copy(q).wait_send()


def spread_kernel(message, messages, send, pass_send, recv):
    me, size = lax.axis_index("tm"), lax.axis_size("tm")
    chip, core = me // 2, me % 2
    blocks = message.shape[0]
    sibling = me + 1 - 2 * core
    greet("tm")

    def out_copy(slot, q, target):
        return remote(
            message.at[q], messages.at[me, q], send.at[slot, q], recv.at[me, q], "tm", target
        )

    def pass_copy(k, q):
        return remote(
            messages.at[k, q], messages.at[k, q], pass_send.at[k, q], recv.at[k, q], "tm", sibling
        )

    def outgoing(act):
        for p in range(size // 2 - 1, 0, -1):

            @pl.when(jnp.logical_and(me >= 1, chip < p))
            def _():
                for q in range(blocks):
                    act(out_copy(p, q, 2 * p + core))

        @pl.when(jnp.logical_and(me >= 2, core == 0))
        def _():
            for q in range(blocks):
                act(out_copy(0, q, me + 1))

    outgoing(lambda copy: copy.start())
    for k in range(1, size - 1):

        @pl.when(me > k)
        def _():
            for q in range(blocks):
                pass_copy(k, q).wait_recv()

                @pl.when(jnp.logical_and(chip > k // 2, core == k % 2))
                def _():
                    pass_copy(k, q).start()

    for k in range(1, size - 1):

        @pl.when(jnp.logical_and(chip > k // 2, core == k % 2))
        def _():
            for q in range(blocks):
                pass_copy(k, q).wait_send()

    outgoing(lambda copy: copy.wait_send())


def transfer(kernel, cid, arrays, outs, scratch):
    return pl.pallas_call(
        kernel,
        out_shape=outs,
        in_specs=[pl.BlockSpec(memory_space=VMEM)] * len(arrays),
        out_specs=jax.tree.map(lambda _: pl.BlockSpec(memory_space=VMEM), outs),
        scratch_shapes=scratch,
        compiler_params=pltpu.CompilerParams(collective_id=cid, has_side_effects=True),
    )(*arrays)


def run_phase(kernel, consts, scalars, arrays, out_shape, scratch):
    smem, vmem = pl.BlockSpec(memory_space=SMEM), pl.BlockSpec(memory_space=VMEM)
    specs = [smem if name in IN_SMEM else vmem for name in CONSTS]
    specs += [smem] * len(scalars) + [vmem] * len(arrays)
    return pl.pallas_call(
        kernel,
        out_shape=out_shape,
        in_specs=specs,
        out_specs=jax.tree.map(lambda _: vmem, out_shape),
        scratch_shapes=scratch,
        compiler_params=pltpu.CompilerParams(vmem_limit_bytes=60 * 1024 * 1024),
    )(*consts, *scalars, *arrays)


def body(
    coarse_guess,
    initial_state,
    fine_volume,
    coarse_volume,
    lift_matrix,
    wave_speed,
    reaction_rate,
    species_map,
    neighbour_element,
    neighbour_rank,
):
    block, variables, nodes = initial_state.shape
    blocks, rows = lax.axis_size("space"), lax.axis_size("tm")
    row, col = lax.axis_index("tm"), lax.axis_index("space")
    partner = jnp.mod(col + neighbour_rank, blocks) * block + neighbour_element
    partner = jnp.pad(partner, ((0, 0), (0, 128 - partner.shape[1])))
    state = jax.ShapeDtypeStruct((blocks, variables * block, nodes), jnp.bfloat16)
    dma = pltpu.SemaphoreType.DMA
    starts, partners = transfer(
        start_kernel,
        0,
        (coarse_guess, initial_state, partner),
        [state, jax.ShapeDtypeStruct((blocks,) + partner.shape, jnp.int32)],
        [
            VMEM((variables * block, nodes), jnp.bfloat16),
            dma((2, blocks - 1)),
            dma((2, blocks - 1)),
            dma((2,)),
        ],
    )
    table = jnp.asarray(face_tables(SIDE)).astype(jnp.bfloat16)
    consts = (
        table,
        partners,
        lift_matrix,
        fine_volume,
        coarse_volume,
        wave_speed,
        reaction_rate,
        species_map,
    )
    dims = (blocks, variables, block, nodes)
    scratch = phase_scratch(dims, lift_matrix.shape[0])
    relaxed = run_phase(phase_one, consts, (), (starts,), state, scratch)
    second = transfer(
        shift_kernel, 1, (relaxed, starts), state, [dma((blocks,)), dma((blocks,)), dma(())]
    )
    where = jnp.stack([row, col]).astype(jnp.int32)
    corr, message = run_phase(
        phase_two,
        consts,
        (where,),
        (second,),
        [jax.ShapeDtypeStruct(dims, jnp.float32), state],
        scratch,
    )
    messages = transfer(
        spread_kernel,
        2,
        (message,),
        jax.ShapeDtypeStruct((rows,) + state.shape, jnp.bfloat16),
        [dma((rows // 2, blocks)), dma((rows, blocks)), dma((rows, blocks))],
    )
    out = run_phase(
        phase_three,
        consts,
        (where,),
        (second, corr, messages),
        jax.ShapeDtypeStruct((STRIDE, variables, block, nodes), jnp.float32),
        scratch,
    )
    return jnp.transpose(out, (0, 2, 1, 3))


def solution(mesh):
    placed = (
        P("tm", "space", None, None),
        P("space", None, None),
        P(),
        P(),
        P(),
        P(),
        P(),
        P(),
        P("space", None),
        P("space", None),
    )
    return jax.shard_map(
        body, mesh=mesh, in_specs=placed, out_specs=P("tm", "space", None, None), check_vma=False
    )
```

```python
import functools

import jax
import jax.numpy as jnp
import numpy as np
from jax import lax
from jax.experimental import pallas as pl
from jax.experimental.pallas import tpu as pltpu
from jax.sharding import PartitionSpec as P

SIDE = 8
STRIDE = 4
COARSE_GAIN = 4.0
VMEM = pltpu.VMEM
SMEM = pltpu.SMEM
MESH = pl.DeviceIdType.MESH


def face_tables(side):
    plane = side * side
    inner = np.arange(plane)
    first, second = inner // side, inner % side
    last = side - 1
    node_lists = [
        first * side + second,
        last * plane + first * side + second,
        first * plane + second,
        first * plane + last * side + second,
        first * plane + second * side,
        first * plane + second * side + last,
    ]
    table = np.zeros((side**3, 12 * plane), np.float32)
    for f in range(6):
        table[node_lists[f], f * plane + inner] = 1.0
        table[node_lists[f ^ 1], (6 + f) * plane + inner] = 1.0
    return table


def find_jumps(speed, c, x_ref, g_ref, j_ref, dims):
    blocks, variables, block, _ = dims
    elems = blocks * block
    faces = c["table"].shape[1] // 2
    plane = faces // 6
    pair = 2 * plane
    both = jnp.dot(x_ref[...], c["table"][...], preferred_element_type=jnp.float32)
    lane = lax.broadcasted_iota(jnp.int32, (1, pair), 1)
    low = jnp.where(lane < plane, 1.0, 0.0)
    high = 1.0 - low

    def first_row(s, v):
        return (s * variables + v) * block

    for k in range(3):
        for v in range(variables):
            swapped = jnp.concatenate(
                [
                    both[
                        first_row(s, v) : first_row(s, v) + block,
                        faces + k * pair : faces + (k + 1) * pair,
                    ]
                    for s in range(blocks)
                ],
                axis=0,
            )
            cols = slice(v * pair, (v + 1) * pair)
            g_ref[k, 0:elems, cols] = (swapped * low).astype(jnp.bfloat16)
            g_ref[k, elems : 2 * elems, cols] = (swapped * high).astype(jnp.bfloat16)
    for k in range(3):
        across = jnp.dot(c["pick"][k], g_ref[k], preferred_element_type=jnp.float32)
        for s in range(blocks):
            for v in range(0, variables, 2):
                parts = []
                for w in (v, v + 1):
                    rows = first_row(s, w)
                    own = both[rows : rows + block, k * pair : (k + 1) * pair]
                    other = across[s * block : (s + 1) * block, w * pair : (w + 1) * pair]
                    parts.append(speed[w] * (other - own))
                rows = first_row(s, v)
                j_ref[rows : rows + 2 * block, k * pair : (k + 1) * pair] = jnp.concatenate(
                    parts, axis=0
                ).astype(jnp.bfloat16)


def transport_react(gain, volume, c, x_ref, j_ref, m_ref, a_ref):
    h_ref = c["halves"]
    moved = jnp.dot(x_ref[...], volume[...], preferred_element_type=jnp.float32)
    moved = moved + jnp.dot(j_ref[...], c["lift"][...], preferred_element_type=jnp.float32)
    moved = moved.reshape(m_ref.shape)
    m_ref[...] = moved
    a_ref[...] = moved
    h_ref[...] = moved * moved + 0.5
    species, rates = c["species"], c["rates"]
    for r in range(species.shape[1]):
        s0, s1, s2 = species[0, r], species[1, r], species[2, r]
        a, b = m_ref[:, s0], m_ref[:, s1]
        rate = (rates[r] * gain) * (a * b) / (h_ref[:, s0] + h_ref[:, s1])
        a_ref[:, s2] += rate
        a_ref[:, s0] -= rate


def store_state(a_ref, x_ref):
    x_ref[...] = a_ref[...].reshape(x_ref.shape).astype(jnp.bfloat16)


CONSTS = ("table", "partner", "lift", "fine", "coarse", "speed", "rates", "species")
IN_SMEM = ("speed", "rates", "species")


def phase_scratch(dims, faces):
    blocks, variables, block, nodes = dims
    rows, elems = blocks * variables * block, blocks * block
    return [
        VMEM((3, elems, 2 * elems), jnp.bfloat16),
        VMEM(dims, jnp.float32),
        VMEM((rows, nodes), jnp.bfloat16),
        VMEM((3, 2 * elems, variables * (faces // 3)), jnp.bfloat16),
        VMEM((rows, faces), jnp.bfloat16),
        VMEM(dims, jnp.float32),
        VMEM(dims, jnp.float32),
    ]


def make_pick(partner_ref, pick_ref):
    _, elems, wide = pick_ref.shape
    blocks, block, _ = partner_ref.shape
    lane = lax.broadcasted_iota(jnp.int32, (block, wide), 1)
    for s in range(blocks):
        partner = partner_ref[s]
        for k in range(3):
            low, high = partner[:, 2 * k : 2 * k + 1], partner[:, 2 * k + 1 : 2 * k + 2]
            wanted = jnp.where(lane < elems, low, high + elems)
            hot = jnp.where(lane == wanted, 1.0, 0.0)
            pick_ref[k, s * block : (s + 1) * block, :] = hot.astype(jnp.bfloat16)


def begin(refs, count):
    c = dict(zip(CONSTS, refs))
    others = refs[len(CONSTS) : len(CONSTS) + count]
    scratch = refs[len(CONSTS) + count :]
    c["pick"], c["halves"] = scratch[:2]
    make_pick(c["partner"], c["pick"])
    return c, others, scratch[2:]


def fine_substep(c, x, g, j, m, a):
    find_jumps(c["speed"], c, x, g, j, m.shape)
    fine_rest(c, x, j, m, a)


def fine_rest(c, x, j, m, a):
    transport_react(1.0, c["fine"], c, x, j, m, a)
    store_state(a, x)


def loop(count, fn):
    def one(i, carry):
        fn(i)
        return carry

    lax.fori_loop(0, count, one, 0)


def phase_one(*refs):
    c, (start, out), (x, g, j, m, a) = begin(refs, 2)
    x[...] = start[...].reshape(x.shape)
    loop(2 * STRIDE, lambda i: fine_substep(c, x, g, j, m, a))
    out[...] = x[...].reshape(out.shape)


def phase_two(*refs):
    c, (second, corr, message), (x, g, j, m, a) = begin(refs, 3)
    x[...] = second[...].reshape(x.shape)
    find_jumps(c["speed"], c, x, g, j, m.shape)
    transport_react(COARSE_GAIN, c["coarse"], c, x, j, m, a)
    corr[...] = a[...]
    fine_rest(c, x, j, m, a)
    loop(2 * STRIDE - 1, lambda i: fine_substep(c, x, g, j, m, a))
    keep = jnp.where(lax.axis_index("tm") == 1, 0.0, 1.0)
    message[...] = (a[...] - keep * corr[...]).reshape(message.shape).astype(jnp.bfloat16)
    corr[...] = a[...] - corr[...]


def phase_three(*refs):
    c, (second, corr, messages, out), (x, g, j, m, a) = begin(refs, 4)
    here, own = lax.axis_index("tm"), lax.axis_index("space")

    @pl.when(here < 2)
    def _():
        x[...] = second[...].reshape(x.shape)

    @pl.when(here >= 2)
    def _():
        x[...] = messages[1].reshape(x.shape)

    def coarse():
        find_jumps(c["speed"], c, x, g, j, m.shape)
        transport_react(COARSE_GAIN, c["coarse"], c, x, j, m, a)

    def advance(i, carry):
        coarse()
        x[...] = (
            a[...].reshape(x.shape) + messages[i].reshape(x.shape).astype(jnp.float32)
        ).astype(jnp.bfloat16)
        return carry

    lax.fori_loop(2, here, advance, 0)
    coarse()
    out[STRIDE - 1] = a[own] + corr[own]

    fine_rest(c, x, j, m, a)

    def point(i):
        fine_substep(c, x, g, j, m, a)

        @pl.when(i % 2 == 0)
        def _():
            out[i // 2] = a[own]

    loop(2 * (STRIDE - 1) - 1, point)


def greet(axis):
    me, size = lax.axis_index(axis), lax.axis_size(axis)
    barrier = pltpu.get_barrier_semaphore()
    for d in range(1, size):
        pl.semaphore_signal(
            barrier, inc=1, device_id={axis: lax.rem(me + d, size)}, device_id_type=MESH
        )
    pl.semaphore_wait(barrier, size - 1)


def remote(src, dst, send, recv, axis, target):
    return pltpu.make_async_remote_copy(
        src_ref=src,
        dst_ref=dst,
        send_sem=send,
        recv_sem=recv,
        device_id={axis: target},
        device_id_type=MESH,
    )


def start_kernel(
    guess, initial, element, rank, starts, partners, mine, partner, send, recv, local
):
    me, size = lax.axis_index("space"), lax.axis_size("space")
    variables, block, _ = initial.shape
    first = lax.axis_index("tm") == 0
    partner[...] = jnp.zeros(partner.shape, jnp.int32)
    other = lax.rem(me + rank[...] + size, size) * block + element[...]
    partner[:, 0 : other.shape[1]] = other

    def take(ref):
        for v in range(0, variables, 2):
            both = jnp.concatenate([ref[v], ref[v + 1]], axis=0)
            mine[v * block : (v + 2) * block, :] = both.astype(jnp.bfloat16)

    @pl.when(first)
    def _():
        take(initial)

    @pl.when(jnp.logical_not(first))
    def _():
        take(guess.at[0])

    greet("space")
    pairs = ((mine, starts), (partner, partners))
    copies = []
    for d in range(1, size):
        for i, (src, dst) in enumerate(pairs):
            copies.append(
                remote(
                    src,
                    dst.at[me],
                    send.at[i, d - 1],
                    recv.at[i, d - 1],
                    "space",
                    lax.rem(me + d, size),
                )
            )
            copies[-1].start()
    for i, (src, dst) in enumerate(pairs):
        copies.append(pltpu.make_async_copy(src, dst.at[me], local.at[i]))
        copies[-1].start()
    for copy in copies:
        copy.wait()


def shift_kernel(relaxed, starts, second, send, recv, local):
    me, size = lax.axis_index("tm"), lax.axis_size("tm")
    blocks = relaxed.shape[0]
    greet("tm")

    def copy(q):
        target = lax.rem(me + 1, size)
        return remote(relaxed.at[q], second.at[q], send.at[q], recv.at[q], "tm", target)

    keep = pltpu.make_async_copy(starts, second, local)

    @pl.when(me < size - 1)
    def _():
        for q in range(blocks):
            copy(q).start()

    @pl.when(me == 0)
    def _():
        keep.start()
        keep.wait()

    @pl.when(me > 0)
    def _():
        for q in range(blocks):
            copy(q).wait_recv()

    @pl.when(me < size - 1)
    def _():
        for q in range(blocks):
            copy(q).wait_send()


def spread_kernel(message, messages, send, pass_send, recv):
    me, size = lax.axis_index("tm"), lax.axis_size("tm")
    chip, core = me // 2, me % 2
    blocks = message.shape[0]
    sibling = me + 1 - 2 * core
    greet("tm")

    def out_copy(slot, q, target):
        return remote(
            message.at[q], messages.at[me, q], send.at[slot, q], recv.at[me, q], "tm", target
        )

    def pass_copy(k, q):
        return remote(
            messages.at[k, q], messages.at[k, q], pass_send.at[k, q], recv.at[k, q], "tm", sibling
        )

    def outgoing(act):
        for p in range(size // 2 - 1, 0, -1):

            @pl.when(jnp.logical_and(me >= 1, chip < p))
            def _():
                for q in range(blocks):
                    act(out_copy(p, q, 2 * p + core))

        @pl.when(jnp.logical_and(me >= 2, core == 0))
        def _():
            for q in range(blocks):
                act(out_copy(0, q, me + 1))

    outgoing(lambda copy: copy.start())
    for k in range(1, size - 1):

        @pl.when(me > k)
        def _():
            for q in range(blocks):
                pass_copy(k, q).wait_recv()

                @pl.when(jnp.logical_and(chip > k // 2, core == k % 2))
                def _():
                    pass_copy(k, q).start()

    for k in range(1, size - 1):

        @pl.when(jnp.logical_and(chip > k // 2, core == k % 2))
        def _():
            for q in range(blocks):
                pass_copy(k, q).wait_send()

    outgoing(lambda copy: copy.wait_send())


def transfer(kernel, cid, arrays, outs, scratch):
    return pl.pallas_call(
        kernel,
        out_shape=outs,
        in_specs=[pl.BlockSpec(memory_space=VMEM)] * len(arrays),
        out_specs=jax.tree.map(lambda _: pl.BlockSpec(memory_space=VMEM), outs),
        scratch_shapes=scratch,
        compiler_params=pltpu.CompilerParams(collective_id=cid, has_side_effects=True),
    )(*arrays)


def run_phase(kernel, consts, scalars, arrays, out_shape, scratch):
    smem, vmem = pl.BlockSpec(memory_space=SMEM), pl.BlockSpec(memory_space=VMEM)
    specs = [smem if name in IN_SMEM else vmem for name in CONSTS]
    specs += [smem] * len(scalars) + [vmem] * len(arrays)
    return pl.pallas_call(
        kernel,
        out_shape=out_shape,
        in_specs=specs,
        out_specs=jax.tree.map(lambda _: vmem, out_shape),
        scratch_shapes=scratch,
        compiler_params=pltpu.CompilerParams(vmem_limit_bytes=60 * 1024 * 1024),
    )(*consts, *scalars, *arrays)


def body(
    coarse_guess,
    initial_state,
    fine_volume,
    coarse_volume,
    lift_matrix,
    wave_speed,
    reaction_rate,
    species_map,
    neighbour_element,
    neighbour_rank,
):
    block, variables, nodes = initial_state.shape
    blocks, rows = lax.axis_size("space"), lax.axis_size("tm")
    state = jax.ShapeDtypeStruct((blocks, variables * block, nodes), jnp.bfloat16)
    dma = pltpu.SemaphoreType.DMA
    starts, partners = transfer(
        start_kernel,
        0,
        (
            jnp.transpose(coarse_guess, (0, 2, 1, 3)),
            jnp.transpose(initial_state, (1, 0, 2)),
            neighbour_element,
            neighbour_rank,
        ),
        [state, jax.ShapeDtypeStruct((blocks, block, 128), jnp.int32)],
        [
            VMEM((variables * block, nodes), jnp.bfloat16),
            VMEM((block, 128), jnp.int32),
            dma((2, blocks - 1)),
            dma((2, blocks - 1)),
            dma((2,)),
        ],
    )
    table = jnp.asarray(face_tables(SIDE)).astype(jnp.bfloat16)
    consts = (
        table,
        partners,
        lift_matrix,
        fine_volume,
        coarse_volume,
        wave_speed,
        reaction_rate,
        jnp.transpose(species_map),
    )
    dims = (blocks, variables, block, nodes)
    scratch = phase_scratch(dims, lift_matrix.shape[0])
    relaxed = run_phase(phase_one, consts, (), (starts,), state, scratch)
    second = transfer(
        shift_kernel, 1, (relaxed, starts), state, [dma((blocks,)), dma((blocks,)), dma(())]
    )
    corr, message = run_phase(
        phase_two,
        consts,
        (),
        (second,),
        [jax.ShapeDtypeStruct(dims, jnp.float32), state],
        scratch,
    )
    messages = transfer(
        spread_kernel,
        2,
        (message,),
        jax.ShapeDtypeStruct((rows,) + state.shape, jnp.bfloat16),
        [dma((rows // 2, blocks)), dma((rows, blocks)), dma((rows, blocks))],
    )
    out = run_phase(
        phase_three,
        consts,
        (),
        (second, corr, messages),
        jax.ShapeDtypeStruct((STRIDE, variables, block, nodes), jnp.float32),
        scratch,
    )
    return jnp.transpose(out, (0, 2, 1, 3))


def solution(mesh):
    placed = (
        P("tm", "space", None, None),
        P("space", None, None),
        P(),
        P(),
        P(),
        P(),
        P(),
        P(),
        P("space", None),
        P("space", None),
    )
    return jax.shard_map(
        body, mesh=mesh, in_specs=placed, out_specs=P("tm", "space", None, None), check_vma=False
    )
```
